32 devices in a mesh: tile: 4 (over y, core), slab: 8 (over z, x).
Axes of the slice: x: 2, y: 2, z: 4, core: 2. Of those that a mesh axis runs over, the one named last changes fastest.
Arguments:
- volume: float32 [256, 16384], P('slab', 'tile'), may hold values from -6 to 6
- measured: float32 [256, 8192], P('slab', 'tile'), may hold values from -6 to 6
- weights: float32 [256, 8192], P('slab', 'tile'), may hold values from 0.25 to 4
- footprints: float32 [1024, 32, 128], P('tile'), may hold values from -0.25 to 0.25
- foot_pixel: int32 [1024], P('tile'), may hold values from 0 to 31
- foot_strip: int32 [1024], P('tile'), may hold values from 0 to 255
Outputs:
- smoothed: float32 [256, 16384], P('slab', 'tile')
- residual: float32 [256, 8192], P('slab', 'tile')
The draws below stay inside these ranges and needn't reach their ends.
Inputs may be any that keep to these rules, and one draw needn't show every extreme that they name: foot_pixel names one of the 32 pixel blocks of the tile that holds the footprint block. foot_strip names a strip of 32 rays.
All inputs are finite; a program needn't handle non-finite values.
Results may differ from the reference program's by a relative error of at most 0.0003.
Values sent between devices are 32-bit elements; how exact they have to be, the bound alone decides.
A program may use at most 64 MiB of HBM per device.

```python
import math
import jax
import jax.numpy as jnp
import numpy as np
from jax import lax

STEPS = 2
PASSES = 3
PB_DEV = 32
FB_DEV = 256
FOOT = 1024
PIX = 16384
SLICES = 256
RAYS = 8192
STRIPS = 256
N_TILE = 4


def with_ends(entries, key, smallest, largest):
    longest = entries.shape.index(max(entries.shape))
    spots = []
    for shift in (0, 1):
        where = [jax.random.randint(jax.random.fold_in(key, axis), (), 0, length) for axis, length in enumerate(entries.shape)]
        where[longest] = (where[longest] + shift) % entries.shape[longest]
        spots.append(tuple(where))
    return entries.at[spots[0]].set(smallest).at[spots[1]].set(largest)


def levels(rng, extent, cuts, low, high):
    gain, own = 1.0, jax.random.fold_in(rng, 6)
    for dim, parts in cuts:
        steps = jnp.exp(jax.random.uniform(jax.random.fold_in(own, dim), (parts,), jnp.float32, low / len(cuts), high / len(cuts)))
        gain = gain * jnp.repeat(steps, extent[dim] // parts).reshape([-1 if axis == dim else 1 for axis in range(len(extent))])
    return gain


def cumulative_ranks(count, lean):
    portions = [(1 << 20) // math.isqrt(grade ** lean) + 1 for grade in range(1, count + 1)]
    deviation = 1 + sum(portions) // (1 << 30)
    return np.cumsum(np.array([max(1, weight // deviation) for weight in portions]))


def ranked_ids(key, dims, number_of, skew):
    listing = cumulative_ranks(number_of, skew)
    lot = jax.random.randint(jax.random.fold_in(key, 1), dims, 0, int(listing[number_of - 1]))
    rank = jnp.searchsorted(jnp.asarray(listing, jnp.int32), lot, side="right")
    return jax.random.permutation(jax.random.fold_in(key, 2), number_of)[rank].astype(jnp.int32)


def normal_values(stream_key, extent, deviation, limit, split=(), kind=jnp.bfloat16):
    values = jax.random.normal(stream_key, extent, jnp.float32) * deviation
    if len(split) > 0:
        values = levels(stream_key, extent, split, -0.22, 0.18) * values
    return jnp.clip(values, min=-limit, max=limit).astype(kind)


def setup_inputs(seed: int = 0) -> dict:
    arg_keys = jax.random.split(jax.random.key(seed), 7)
    volume = normal_values(arg_keys[0], (SLICES, PIX), 1.0, 6.0, ((0, 8), (1, 4)), jnp.float32)
    measured = normal_values(arg_keys[1], (SLICES, RAYS), 1.0, 6.0, ((0, 8), (1, 4)), jnp.float32)
    weights = jnp.clip(jnp.exp(math.log(4.0) - 2.7725887 * jax.random.uniform(arg_keys[2], (SLICES, RAYS), jnp.float32) ** levels(arg_keys[2], (SLICES, RAYS), ((0, 8), (1, 4)), -0.2, 0.2)), 0.25, 4.0)
    footprints = normal_values(arg_keys[3], (FOOT, 32, 128), (128 * FOOT // STRIPS) ** -0.5, 0.25, ((0, 4),), jnp.float32)
    foot_pixel = with_ends(jax.random.randint(arg_keys[4], (FOOT,), 0, PB_DEV), jax.random.fold_in(arg_keys[4], 1), 0, PB_DEV - 1).astype(jnp.int32)
    foot_strip = with_ends(ranked_ids(arg_keys[5], (FOOT,), STRIPS, 2), jax.random.fold_in(arg_keys[5], 3), 0, STRIPS - 1).astype(jnp.int32)
    return dict(volume=volume, measured=measured, weights=weights, footprints=footprints, foot_pixel=foot_pixel, foot_strip=foot_strip)


huber_width = 0.5
smooth_rate = 0.2
highest = lax.Precision.HIGHEST


def tile_project(blocked, blocks, pixel_ids, strip_ids):
    picked = jnp.take(blocked, pixel_ids, axis=1)
    contrib = jnp.einsum("sbj,bkj->sbk", picked, blocks, precision=highest)
    strip_hot = (strip_ids[:, None] == jnp.arange(STRIPS, dtype=jnp.int32)[None, :]).astype(jnp.float32)
    summed = jnp.einsum("sbk,bq->sqk", contrib, strip_hot, precision=highest)
    return summed.reshape(summed.shape[0], STRIPS * 32)


def tile_back(ray_values, blocks, pixel_ids, strip_ids, pixel_count):
    strip_rows = ray_values.reshape(ray_values.shape[0], STRIPS, 32)
    strip_hot = (strip_ids[:, None] == jnp.arange(STRIPS, dtype=jnp.int32)[None, :]).astype(jnp.float32)
    picked = jnp.einsum("sqk,bq->sbk", strip_rows, strip_hot, precision=highest)
    spread = jnp.einsum("sbk,bkj->sbj", picked, blocks, precision=highest)
    pixel_hot = (pixel_ids[:, None] == jnp.arange(pixel_count, dtype=jnp.int32)[None, :]).astype(jnp.float32)
    placed = jnp.einsum("sbj,bp->spj", spread, pixel_hot, precision=highest)
    return placed.reshape(ray_values.shape[0], pixel_count * 128)


def forward_all(field, footprints, foot_pixel, foot_strip):
    tiled = jnp.moveaxis(field.reshape(SLICES, N_TILE, PB_DEV, 128), 1, 0)
    blocks = footprints.reshape(N_TILE, FB_DEV, 32, 128)
    pixels = foot_pixel.reshape(N_TILE, FB_DEV)
    strips = foot_strip.reshape(N_TILE, FB_DEV)

    def add_tile(total, pieces):
        return total + tile_project(pieces[0], pieces[1], pieces[2], pieces[3]), None

    start_sum = jnp.zeros((SLICES, RAYS), jnp.float32)
    return lax.scan(add_tile, start_sum, (tiled, blocks, pixels, strips))[0]


def backward_all(ray_values, footprints, foot_pixel, foot_strip):
    blocks = footprints.reshape(N_TILE, FB_DEV, 32, 128)
    pixels = foot_pixel.reshape(N_TILE, FB_DEV)
    strips = foot_strip.reshape(N_TILE, FB_DEV)

    def one_tile(pieces):
        return tile_back(ray_values, pieces[0], pieces[1], pieces[2], PB_DEV)

    stacked = lax.map(one_tile, (blocks, pixels, strips))
    return jnp.moveaxis(stacked, 0, 1).reshape(SLICES, PIX)


def reference(volume, measured, weights, footprints, foot_pixel, foot_strip):
    residual = forward_all(volume, footprints, foot_pixel, foot_strip) - measured
    current = volume
    for number in range(STEPS):
        gradient = backward_all(weights * residual, footprints, foot_pixel, foot_strip)
        projected = forward_all(gradient, footprints, foot_pixel, foot_strip)
        grad_total = jnp.sum(gradient * gradient)
        curve_total = jnp.sum(weights * projected * projected)
        step_size = grad_total / curve_total
        current = current - step_size * gradient
        residual = residual - step_size * projected
    zero_row = jnp.zeros((1, current.shape[1]), jnp.float32)
    for number in range(PASSES):
        clipped = jnp.clip(current[1:] - current[:-1], -huber_width, huber_width)
        upper = jnp.concatenate([clipped, zero_row], axis=0)
        lower = jnp.concatenate([zero_row, clipped], axis=0)
        current = current + smooth_rate * (upper - lower)
    return current, residual
```

```python
import functools

import jax
import jax.numpy as jnp
from jax import lax
from jax.experimental import pallas as pl
from jax.experimental.pallas import tpu as pltpu
from jax.sharding import PartitionSpec as P

STRIPS = 256
PASSES = 3
LANES = 128
UNROLL = 8
MOST_CHUNKS = 4

huber_width = 0.5
smooth_rate = 0.2
MESH = pl.DeviceIdType.MESH
VMEM = pl.BlockSpec(memory_space=pltpu.VMEM)
SMEM = pl.BlockSpec(memory_space=pltpu.SMEM)
f32 = jnp.float32
bf16 = jnp.bfloat16


def halves(x):
    high = x.astype(bf16)
    return high, (x - high.astype(f32)).astype(bf16)


def triple(x):
    high, low = halves(x)
    return jnp.concatenate([high, low, high], axis=1)


def project(v3, fs, pix, strip, part):
    count, rows, _ = fs.shape
    slots = LANES // rows
    slices = v3.shape[1]
    slot_of = lax.broadcasted_iota(jnp.int32, (slices, LANES), 1) // rows
    part[...] = jnp.zeros_like(part)

    def step(i, carry):
        found = []
        for u in range(UNROLL):
            b = i * UNROLL + u
            q = strip[b]
            pair = fs[b]
            high, low = pair[:, :LANES], pair[:, LANES:]
            right = jnp.concatenate([jnp.concatenate([high, high, low], axis=1)] * slots, axis=0)
            out = lax.dot_general(
                v3[pix[b]], right, (((1,), (1,)), ((), ())), preferred_element_type=f32
            )
            found.append((q, jnp.where(slot_of == q % slots, out, 0.0)))
        for q, out in found:
            part[q // slots] += out
        return carry

    lax.fori_loop(0, count // UNROLL, step, 0)


def back(r3, mask, fs, pix, strip, grad):
    count, rows, _ = fs.shape
    slots = LANES // rows
    grad[...] = jnp.zeros_like(grad)

    def step(i, carry):
        found = []
        for u in range(UNROLL):
            b = i * UNROLL + u
            q = strip[b]
            pair = fs[b]
            high, low = pair[:, :LANES], pair[:, LANES:]
            right = jnp.concatenate([high] * (2 * slots) + [low] * slots, axis=0)
            left = r3[q // slots] * mask[q % slots]
            out = lax.dot_general(
                left, right, (((1,), (0,)), ((), ())), preferred_element_type=f32
            )
            found.append((pix[b], out))
        for p, out in found:
            grad[p] += out
        return carry

    lax.fori_loop(0, count // UNROLL, step, 0)


def fill_mask(mask, rows):
    slots, slices, wide = mask.shape
    slot_of = (lax.broadcasted_iota(jnp.int32, (slices, wide), 1) % LANES) // rows
    for slot in range(slots):
        mask[slot] = jnp.where(slot_of == slot, 1.0, 0.0).astype(bf16)


def first_kernel(pix, strip, volume, feet, fs, part, v3):
    count = feet.shape[0]
    for p in range(v3.shape[0]):
        v3[p] = triple(volume[:, p * LANES : (p + 1) * LANES])

    def split(i, carry):
        for u in range(UNROLL):
            b = i * UNROLL + u
            fs[b] = jnp.concatenate(halves(feet[b]), axis=1)
        return carry

    lax.fori_loop(0, count // UNROLL, split, 0)
    project(v3, fs, pix, strip, part)


def fold8(x):
    return jnp.sum(x.reshape(x.shape[0] // 8, 8, LANES), axis=0)


def load_rays(wr, r3):
    def one(g, carry):
        r3[g] = triple(wr[g])
        return carry

    lax.fori_loop(0, r3.shape[0], one, 0)


def middle_kernel(pix, strip, fs, wr, grad, part, square, v3, r3, mask):
    fill_mask(mask, fs.shape[1])
    load_rays(wr, r3)
    back(r3, mask, fs, pix, strip, grad)
    total = jnp.zeros((8, LANES), f32)
    for p in range(v3.shape[0]):
        value = grad[p]
        v3[p] = triple(value)
        total += fold8(value * value)
    square[...] = total
    project(v3, fs, pix, strip, part)


def last_kernel(pix, strip, fs, wr, first, volume, sums, grad, part, square, current, halo, v3, r3, mask):
    fill_mask(mask, fs.shape[1])
    load_rays(wr, r3)
    back(r3, mask, fs, pix, strip, grad)
    rate = jnp.sum(sums[0]) / jnp.sum(sums[1])
    slices = grad.shape[1]
    total = jnp.zeros((8, LANES), f32)
    for p in range(v3.shape[0]):
        value = first[p] - rate * grad[p]
        now = volume[:, p * LANES : (p + 1) * LANES] - rate * first[p]
        grad[p] = value
        current[p] = now
        v3[p] = triple(value)
        total += fold8(value * value)
    square[...] = total
    for which, source in enumerate((current, grad)):
        for row in range(PASSES):
            halo[0, which, row] = source[:, slices - PASSES + row, :]
            halo[1, which, row] = source[:, row, :]
    project(v3, fs, pix, strip, part)


def finish_kernel(current, grad, halo, sums, rate_sums, start, projected, later, smoothed, residual, ext):
    rate0 = jnp.sum(rate_sums[0]) / jnp.sum(rate_sums[1])
    rate1 = jnp.sum(sums[0]) / jnp.sum(sums[1])
    count, slices, _ = current.shape
    for g in range(start.shape[0]):
        residual[:, g * LANES : (g + 1) * LANES] = (
            start[g] - rate0 * projected[g] - rate1 * later[g]
        )
    tall = slices + 16
    first_row = lax.axis_index("slab") * slices - 8
    total_rows = slices * lax.axis_size("slab")
    row = first_row + lax.broadcasted_iota(jnp.int32, (tall, LANES), 0)
    linked = (row >= 0) & (row + 1 < total_rows)
    for p in range(count):
        ext[p, 0:8] = jnp.zeros((8, LANES), f32)
        ext[p, 8 : 8 + slices] = current[p] - rate1 * grad[p]
        ext[p, 8 + slices :] = jnp.zeros((8, LANES), f32)
    for i in range(PASSES):
        ext[:, 8 - PASSES + i, :] = halo[0, 0, i] - rate1 * halo[0, 1, i]
        ext[:, 8 + slices + i, :] = halo[1, 0, i] - rate1 * halo[1, 1, i]
    for p in range(count):
        value = ext[p]
        for number in range(PASSES):
            differ = jnp.clip(pltpu.roll(value, tall - 1, 0) - value, -huber_width, huber_width)
            clipped = jnp.where(linked, differ, 0.0)
            value = value + smooth_rate * (clipped - pltpu.roll(clipped, 1, 0))
        smoothed[:, p * LANES : (p + 1) * LANES] = value[8 : 8 + slices]


def exchange_kernel(mode, n, slabs, chunks, *refs):
    refs = list(refs)
    part = refs.pop(0)
    weights = refs.pop(0)
    measured = refs.pop(0) if mode == "first" else None
    square = refs.pop(0) if mode != "first" else None
    halo = refs.pop(0) if mode == "last" else None
    own = refs.pop(0)
    gathered = refs.pop(0) if mode != "last" else None
    sums = refs.pop(0) if mode != "first" else None
    halo_in = refs.pop(0) if mode == "last" else None
    near, chip_sum, far, near_s, near_r, far_s, far_r, ag_s, ag_r, sib_s, sib_r = refs[:11]
    refs = refs[11:]
    if mode != "first":
        mine, tile_in, slab_in, t_s, t_r, b_s, b_r = refs[:7]
        refs = refs[7:]
    if mode == "last":
        h_s, h_r = refs

    half = n // 2
    pieces = part.shape[2]
    size = pieces // chunks
    me = lax.axis_index("tile")
    slab = lax.axis_index("slab")
    par = lax.rem(me, 2)
    row = me // 2
    sibling = me + 1 - 2 * par
    started = []

    def at(tile):
        return {"tile": tile}

    def along(other):
        return {"slab": other}

    def peer(d):
        return lax.rem(row + d, half) * 2 + par

    def send(src, dst, s, r, where):
        copy = pltpu.make_async_remote_copy(
            src_ref=src, dst_ref=dst, send_sem=s, recv_sem=r, device_id=where, device_id_type=MESH
        )
        copy.start()
        started.append(copy)
        return copy

    barrier = pltpu.get_barrier_semaphore()
    greeted = 0
    if mode == "first":
        tiles = [sibling] + [peer(d) for d in range(1, half)]
    else:
        tiles = [lax.rem(me + d, n) for d in range(1, n)]
    for tile in tiles:
        pl.semaphore_signal(barrier, inc=1, device_id=at(tile), device_id_type=MESH)
        greeted += 1
    if mode != "first":
        for d in range(1, slabs):
            pl.semaphore_signal(
                barrier, inc=1, device_id=along(lax.rem(slab + d, slabs)), device_id_type=MESH
            )
            greeted += 1
    pl.semaphore_wait(barrier, greeted)

    spans = [pl.ds(c * size, size) for c in range(chunks)]
    first_hop = [
        send(part.at[:, 1 - par, span], near.at[:, span], near_s.at[c], near_r.at[c], at(sibling))
        for c, span in enumerate(spans)
    ]
    second_hop = []
    for c, span in enumerate(spans):
        first_hop[c].wait_recv()
        for g in range(c * size, (c + 1) * size):
            for o in range(half):
                chip_sum[o, g] = part[o, par, g] + near[o, g]
        second_hop.append(
            [
                send(
                    chip_sum.at[lax.rem(row + d, half), span],
                    far.at[d - 1, span],
                    far_s.at[c, d - 1],
                    far_r.at[c, d - 1],
                    at(peer(d)),
                )
                for d in range(1, half)
            ]
        )
    if mode == "last":
        up = send(halo.at[0], halo_in.at[0], h_s.at[0], h_r.at[0], along(lax.rem(slab + 1, slabs)))
        down = send(
            halo.at[1], halo_in.at[1], h_s.at[1], h_r.at[1], along(lax.rem(slab + slabs - 1, slabs))
        )
    curve = jnp.zeros((8, LANES), f32)
    across = []
    aside = []
    for c, span in enumerate(spans):
        for copy in second_hop[c]:
            copy.wait_recv()
        for g in range(c * size, (c + 1) * size):
            value = chip_sum[row, g]
            for d in range(1, half):
                value += far[d - 1, g]
            lanes = slice(g * LANES, (g + 1) * LANES)
            if mode == "first":
                value = value - measured[:, lanes]
            weighted = weights[:, lanes] * value
            own[g] = value
            if mode != "first":
                curve += fold8(weighted * value)
            if mode != "last":
                gathered[row, par, g] = weighted
        if mode != "last":
            spot = gathered.at[row, par, span]
            across.append(
                [
                    send(spot, spot, ag_s.at[c, d - 1], ag_r.at[c, d - 1], at(peer(d)))
                    for d in range(1, half)
                ]
            )
            aside.append(send(spot, spot, sib_s.at[0, c], sib_r.at[0, c], at(sibling)))
    if mode != "first":
        mine[0, 0] = square[...]
        mine[0, 1] = curve
        tile_copies = [
            send(
                mine.at[0],
                tile_in.at[d - 1],
                t_s.at[d - 1],
                t_r.at[d - 1],
                at(lax.rem(me + d, n)),
            )
            for d in range(1, n)
        ]
    if mode != "last":
        for c, span in enumerate(spans):
            for d in range(1, half):
                across[c][d - 1].wait_recv()
                spot = gathered.at[lax.rem(row + half - d, half), par, span]
                aside.append(send(spot, spot, sib_s.at[d, c], sib_r.at[d, c], at(sibling)))
    if mode != "first":
        total = mine[0]
        for d in range(1, n):
            tile_copies[d - 1].wait_recv()
            total += tile_in[d - 1]
        mine[1] = total
        slab_copies = [
            send(
                mine.at[1],
                slab_in.at[d - 1],
                b_s.at[d - 1],
                b_r.at[d - 1],
                along(lax.rem(slab + d, slabs)),
            )
            for d in range(1, slabs)
        ]
        for d in range(1, slabs):
            slab_copies[d - 1].wait_recv()
            total += slab_in[d - 1]
        sums[...] = total
    for copy in aside:
        copy.wait_recv()
    if mode == "last":
        up.wait_recv()
        down.wait_recv()
    for copy in started:
        copy.wait_send()


def exchange(mode, part, weights, extra, n, slabs, ident):
    groups, slices, _ = part.shape
    half, pieces = n // 2, groups // n
    chunks = max(c for c in range(1, MOST_CHUNKS + 1) if pieces % c == 0)
    shape = jax.ShapeDtypeStruct
    outs = [shape((pieces, slices, LANES), f32)]
    if mode != "last":
        outs.append(shape((half, 2, pieces, slices, LANES), f32))
    if mode != "first":
        outs.append(shape((2, 8, LANES), f32))
    if mode == "last":
        outs.append(shape(extra[1].shape, f32))
    dma = pltpu.SemaphoreType.DMA
    others = max(half - 1, 1)
    scratch = [
        pltpu.VMEM((half, pieces, slices, LANES), f32),
        pltpu.VMEM((half, pieces, slices, LANES), f32),
        pltpu.VMEM((others, pieces, slices, LANES), f32),
        dma((chunks,)),
        dma((chunks,)),
        dma((chunks, others)),
        dma((chunks, others)),
        dma((chunks, others)),
        dma((chunks, others)),
        dma((half, chunks)),
        dma((half, chunks)),
    ]
    if mode != "first":
        scratch += [
            pltpu.VMEM((2, 2, 8, LANES), f32),
            pltpu.VMEM((n - 1, 2, 8, LANES), f32),
            pltpu.VMEM((max(slabs - 1, 1), 2, 8, LANES), f32),
            dma((n - 1,)),
            dma((n - 1,)),
            dma((max(slabs - 1, 1),)),
            dma((max(slabs - 1, 1),)),
        ]
    if mode == "last":
        scratch += [dma((2,)), dma((2,))]
    inputs = [part.reshape(half, 2, pieces, slices, LANES), weights, *extra]
    return pl.pallas_call(
        functools.partial(exchange_kernel, mode, n, slabs, chunks),
        out_shape=outs,
        in_specs=[VMEM] * len(inputs),
        out_specs=[VMEM] * len(outs),
        scratch_shapes=scratch,
        compiler_params=pltpu.CompilerParams(collective_id=ident, has_side_effects=True),
        name="exchange_" + mode,
    )(*inputs)


def shards(n, slabs, volume, measured, weights, footprints, foot_pixel, foot_strip):
    slices = volume.shape[0]
    blocks = volume.shape[1] // LANES
    count, rows, _ = footprints.shape
    slots = LANES // rows
    groups = STRIPS // slots
    shape = jax.ShapeDtypeStruct
    part_shape = shape((groups, slices, LANES), f32)
    grad_shape = shape((blocks, slices, LANES), f32)
    v3 = pltpu.VMEM((blocks, slices, 3 * LANES), bf16)
    r3 = pltpu.VMEM((groups, slices, 3 * LANES), bf16)
    mask = pltpu.VMEM((slots, slices, 3 * LANES), bf16)

    def local(body, name, outs, scratch, *inputs):
        return pl.pallas_call(
            body,
            out_shape=outs,
            in_specs=[SMEM, SMEM] + [VMEM] * len(inputs),
            out_specs=[VMEM] * len(outs),
            scratch_shapes=scratch,
            name=name,
        )(foot_pixel, foot_strip, *inputs)

    fs, part = local(
        first_kernel,
        "project_first",
        [shape((count, rows, 2 * LANES), bf16), part_shape],
        [v3],
        volume,
        footprints,
    )
    start, wr = exchange("first", part, weights, [measured], n, slabs, 1)
    first, part, square = local(
        middle_kernel,
        "gradient_first",
        [grad_shape, part_shape, shape((8, LANES), f32)],
        [v3, r3, mask],
        fs,
        wr.reshape(groups, slices, LANES),
    )
    projected, wp, sums = exchange("middle", part, weights, [square], n, slabs, 2)
    halo_shape = shape((2, 2, PASSES, blocks, LANES), f32)
    grad, part, square, current, halo = local(
        last_kernel,
        "gradient_second",
        [grad_shape, part_shape, shape((8, LANES), f32), grad_shape, halo_shape],
        [v3, r3, mask],
        fs,
        wp.reshape(groups, slices, LANES),
        first,
        volume,
        sums,
    )
    later, last_sums, halo_in = exchange("last", part, weights, [square, halo], n, slabs, 3)
    return pl.pallas_call(
        finish_kernel,
        out_shape=[shape(volume.shape, f32), shape(measured.shape, f32)],
        in_specs=[VMEM] * 8,
        out_specs=[VMEM] * 2,
        scratch_shapes=[pltpu.VMEM((blocks, slices + 16, LANES), f32)],
        name="smooth",
    )(current, grad, halo_in, last_sums, sums, start, projected, later)


def solution(mesh):
    return jax.shard_map(
        functools.partial(shards, mesh.shape["tile"], mesh.shape["slab"]),
        mesh=mesh,
        in_specs=(
            P("slab", "tile"),
            P("slab", "tile"),
            P("slab", "tile"),
            P("tile", None, None),
            P("tile"),
            P("tile"),
        ),
        out_specs=(P("slab", "tile"), P("slab", "tile")),
        check_vma=False,
    )
```

```python
import functools

import jax
import jax.numpy as jnp
from jax import lax
from jax.experimental import pallas as pl
from jax.experimental.pallas import tpu as pltpu
from jax.sharding import PartitionSpec as P

STRIPS = 256
PASSES = 3
LANES = 128
UNROLL = 2
MOST_CHUNKS = 4

huber_width = 0.5
smooth_rate = 0.2
MESH = pl.DeviceIdType.MESH
VMEM = pl.BlockSpec(memory_space=pltpu.VMEM)
SMEM = pl.BlockSpec(memory_space=pltpu.SMEM)
f32 = jnp.float32
bf16 = jnp.bfloat16


def halves(x):
    high = x.astype(bf16)
    return high, (x - high.astype(f32)).astype(bf16)


def triple(x):
    high, low = halves(x)
    return jnp.concatenate([high, low, high], axis=1)


def project(v3, fs, pix, strip, part):
    slices = v3.shape[1]
    slots = pix.shape[0] // fs.shape[0]
    rows = LANES // slots
    slot_of = lax.broadcasted_iota(jnp.int32, (slices, LANES), 1) // rows
    part[...] = jnp.zeros_like(part)

    def step(i, carry):
        found = []
        for u in range(UNROLL):
            t = i * UNROLL + u
            pair = fs[t]
            high, low = pair[:, :LANES], pair[:, LANES:]
            right = jnp.concatenate([high, high, low], axis=1)
            left = jnp.concatenate([v3[pix[t * slots + k]] for k in range(slots)], axis=0)
            out = lax.dot_general(
                left, right, (((1,), (1,)), ((), ())), preferred_element_type=f32
            )
            for k in range(slots):
                q = strip[t * slots + k]
                own = q % slots
                turned = pltpu.roll(
                    out[k * slices : (k + 1) * slices], ((own - k + slots) % slots) * rows, 1
                )
                found.append((q // slots, jnp.where(slot_of == own, turned, 0.0)))
        for g, out in found:
            part[g] += out
        return carry

    lax.fori_loop(0, fs.shape[0] // UNROLL, step, 0)


def back(wr, fs, pix, strip, grad):
    slices = wr.shape[1]
    slots = pix.shape[0] // fs.shape[0]
    rows = LANES // slots
    slot_of = lax.broadcasted_iota(jnp.int32, (slices, LANES), 1) // rows
    grad[...] = jnp.zeros_like(grad)

    def step(i, carry):
        found = []
        for u in range(UNROLL):
            t = i * UNROLL + u
            pair = fs[t]
            high, low = pair[:, :LANES], pair[:, LANES:]
            right = jnp.concatenate([high, high, low], axis=0)
            left = []
            for k in range(slots):
                q = strip[t * slots + k]
                turned = pltpu.roll(
                    wr[q // slots], ((k - q % slots + slots) % slots) * rows, 1
                )
                left.append(triple(jnp.where(slot_of == k, turned, 0.0)))
            out = lax.dot_general(
                jnp.concatenate(left, axis=0),
                right,
                (((1,), (0,)), ((), ())),
                preferred_element_type=f32,
            )
            for k in range(slots):
                found.append((pix[t * slots + k], out[k * slices : (k + 1) * slices]))
        for p, out in found:
            grad[p] += out
        return carry

    lax.fori_loop(0, fs.shape[0] // UNROLL, step, 0)


def first_kernel(pix, strip, volume, feet, fs, part, v3):
    for p in range(v3.shape[0]):
        v3[p] = triple(volume[:, p * LANES : (p + 1) * LANES])

    def split(i, carry):
        for u in range(UNROLL):
            t = i * UNROLL + u
            fs[t] = jnp.concatenate(halves(feet[t]), axis=1)
        return carry

    lax.fori_loop(0, feet.shape[0] // UNROLL, split, 0)
    project(v3, fs, pix, strip, part)


def fold8(x):
    return jnp.sum(x.reshape(x.shape[0] // 8, 8, LANES), axis=0)


def middle_kernel(pix, strip, fs, wr, grad, part, square, v3):
    back(wr, fs, pix, strip, grad)
    total = jnp.zeros((8, LANES), f32)
    for p in range(v3.shape[0]):
        value = grad[p]
        v3[p] = triple(value)
        total += fold8(value * value)
    square[...] = total
    project(v3, fs, pix, strip, part)


def last_kernel(pix, strip, fs, wr, first, volume, sums, grad, part, square, current, halo, v3):
    back(wr, fs, pix, strip, grad)
    rate = jnp.sum(sums[0]) / jnp.sum(sums[1])
    slices = grad.shape[1]
    total = jnp.zeros((8, LANES), f32)
    for p in range(v3.shape[0]):
        value = first[p] - rate * grad[p]
        now = volume[:, p * LANES : (p + 1) * LANES] - rate * first[p]
        grad[p] = value
        current[p] = now
        v3[p] = triple(value)
        total += fold8(value * value)
    square[...] = total
    for which, source in enumerate((current, grad)):
        for row in range(PASSES):
            halo[0, which, row] = source[:, slices - PASSES + row, :]
            halo[1, which, row] = source[:, row, :]
    project(v3, fs, pix, strip, part)


def finish_kernel(current, grad, halo, sums, rate_sums, start, projected, later, smoothed, residual, ext):
    rate0 = jnp.sum(rate_sums[0]) / jnp.sum(rate_sums[1])
    rate1 = jnp.sum(sums[0]) / jnp.sum(sums[1])
    count, slices, _ = current.shape
    for g in range(start.shape[0]):
        residual[:, g * LANES : (g + 1) * LANES] = (
            start[g] - rate0 * projected[g] - rate1 * later[g]
        )
    tall = slices + 16
    first_row = lax.axis_index("slab") * slices - 8
    total_rows = slices * lax.axis_size("slab")
    row = first_row + lax.broadcasted_iota(jnp.int32, (tall, LANES), 0)
    linked = (row >= 0) & (row + 1 < total_rows)
    for p in range(count):
        ext[p, 0:8] = jnp.zeros((8, LANES), f32)
        ext[p, 8 : 8 + slices] = current[p] - rate1 * grad[p]
        ext[p, 8 + slices :] = jnp.zeros((8, LANES), f32)
    for i in range(PASSES):
        ext[:, 8 - PASSES + i, :] = halo[0, 0, i] - rate1 * halo[0, 1, i]
        ext[:, 8 + slices + i, :] = halo[1, 0, i] - rate1 * halo[1, 1, i]
    for p in range(count):
        value = ext[p]
        for number in range(PASSES):
            differ = jnp.clip(pltpu.roll(value, tall - 1, 0) - value, -huber_width, huber_width)
            clipped = jnp.where(linked, differ, 0.0)
            value = value + smooth_rate * (clipped - pltpu.roll(clipped, 1, 0))
        smoothed[:, p * LANES : (p + 1) * LANES] = value[8 : 8 + slices]


def exchange_kernel(mode, n, slabs, chunks, *refs):
    refs = list(refs)
    part = refs.pop(0)
    weights = refs.pop(0)
    measured = refs.pop(0) if mode == "first" else None
    square = refs.pop(0) if mode != "first" else None
    halo = refs.pop(0) if mode == "last" else None
    own = refs.pop(0)
    gathered = refs.pop(0) if mode != "last" else None
    sums = refs.pop(0) if mode != "first" else None
    halo_in = refs.pop(0) if mode == "last" else None
    near, chip_sum, far, near_s, near_r, far_s, far_r, ag_s, ag_r, sib_s, sib_r = refs[:11]
    refs = refs[11:]
    if mode != "first":
        mine, tile_in, slab_in, t_s, t_r, b_s, b_r = refs[:7]
        refs = refs[7:]
    if mode == "last":
        h_s, h_r = refs

    half = n // 2
    pieces = part.shape[2]
    size = pieces // chunks
    me = lax.axis_index("tile")
    slab = lax.axis_index("slab")
    par = lax.rem(me, 2)
    row = me // 2
    sibling = me + 1 - 2 * par
    started = []

    def at(tile):
        return {"tile": tile}

    def along(other):
        return {"slab": other}

    def peer(d):
        return lax.rem(row + d, half) * 2 + par

    def send(src, dst, s, r, where):
        copy = pltpu.make_async_remote_copy(
            src_ref=src, dst_ref=dst, send_sem=s, recv_sem=r, device_id=where, device_id_type=MESH
        )
        copy.start()
        started.append(copy)
        return copy

    barrier = pltpu.get_barrier_semaphore()
    greeted = 0
    if mode == "first":
        tiles = [sibling] + [peer(d) for d in range(1, half)]
    else:
        tiles = [lax.rem(me + d, n) for d in range(1, n)]
    for tile in tiles:
        pl.semaphore_signal(barrier, inc=1, device_id=at(tile), device_id_type=MESH)
        greeted += 1
    if mode != "first":
        for d in range(1, slabs):
            pl.semaphore_signal(
                barrier, inc=1, device_id=along(lax.rem(slab + d, slabs)), device_id_type=MESH
            )
            greeted += 1
    pl.semaphore_wait(barrier, greeted)

    spans = [pl.ds(c * size, size) for c in range(chunks)]
    first_hop = [
        send(part.at[:, 1 - par, span], near.at[:, span], near_s.at[c], near_r.at[c], at(sibling))
        for c, span in enumerate(spans)
    ]
    second_hop = []
    for c, span in enumerate(spans):
        first_hop[c].wait_recv()
        for g in range(c * size, (c + 1) * size):
            for o in range(half):
                chip_sum[o, g] = part[o, par, g] + near[o, g]
        second_hop.append(
            [
                send(
                    chip_sum.at[lax.rem(row + d, half), span],
                    far.at[d - 1, span],
                    far_s.at[c, d - 1],
                    far_r.at[c, d - 1],
                    at(peer(d)),
                )
                for d in range(1, half)
            ]
        )
    if mode == "last":
        up = send(halo.at[0], halo_in.at[0], h_s.at[0], h_r.at[0], along(lax.rem(slab + 1, slabs)))
        down = send(
            halo.at[1], halo_in.at[1], h_s.at[1], h_r.at[1], along(lax.rem(slab + slabs - 1, slabs))
        )
    curve = jnp.zeros((8, LANES), f32)
    across = []
    aside = []
    for c, span in enumerate(spans):
        for copy in second_hop[c]:
            copy.wait_recv()
        for g in range(c * size, (c + 1) * size):
            value = chip_sum[row, g]
            for d in range(1, half):
                value += far[d - 1, g]
            lanes = slice(g * LANES, (g + 1) * LANES)
            if mode == "first":
                value = value - measured[:, lanes]
            weighted = weights[:, lanes] * value
            own[g] = value
            if mode != "first":
                curve += fold8(weighted * value)
            if mode != "last":
                gathered[row, par, g] = weighted
        if mode != "last":
            spot = gathered.at[row, par, span]
            across.append(
                [
                    send(spot, spot, ag_s.at[c, d - 1], ag_r.at[c, d - 1], at(peer(d)))
                    for d in range(1, half)
                ]
            )
            aside.append(send(spot, spot, sib_s.at[0, c], sib_r.at[0, c], at(sibling)))
    if mode != "first":
        mine[0, 0] = square[...]
        mine[0, 1] = curve
        tile_copies = [
            send(
                mine.at[0],
                tile_in.at[d - 1],
                t_s.at[d - 1],
                t_r.at[d - 1],
                at(lax.rem(me + d, n)),
            )
            for d in range(1, n)
        ]
    if mode != "last":
        for c, span in enumerate(spans):
            for d in range(1, half):
                across[c][d - 1].wait_recv()
                spot = gathered.at[lax.rem(row + half - d, half), par, span]
                aside.append(send(spot, spot, sib_s.at[d, c], sib_r.at[d, c], at(sibling)))
    if mode != "first":
        total = mine[0]
        for d in range(1, n):
            tile_copies[d - 1].wait_recv()
            total += tile_in[d - 1]
        mine[1] = total
        slab_copies = [
            send(
                mine.at[1],
                slab_in.at[d - 1],
                b_s.at[d - 1],
                b_r.at[d - 1],
                along(lax.rem(slab + d, slabs)),
            )
            for d in range(1, slabs)
        ]
        for d in range(1, slabs):
            slab_copies[d - 1].wait_recv()
            total += slab_in[d - 1]
        sums[...] = total
    for copy in aside:
        copy.wait_recv()
    if mode == "last":
        up.wait_recv()
        down.wait_recv()
    for copy in started:
        copy.wait_send()


def exchange(mode, part, weights, extra, n, slabs, ident):
    groups, slices, _ = part.shape
    half, pieces = n // 2, groups // n
    chunks = max(c for c in range(1, MOST_CHUNKS + 1) if pieces % c == 0)
    shape = jax.ShapeDtypeStruct
    outs = [shape((pieces, slices, LANES), f32)]
    if mode != "last":
        outs.append(shape((half, 2, pieces, slices, LANES), f32))
    if mode != "first":
        outs.append(shape((2, 8, LANES), f32))
    if mode == "last":
        outs.append(shape(extra[1].shape, f32))
    dma = pltpu.SemaphoreType.DMA
    others = max(half - 1, 1)
    scratch = [
        pltpu.VMEM((half, pieces, slices, LANES), f32),
        pltpu.VMEM((half, pieces, slices, LANES), f32),
        pltpu.VMEM((others, pieces, slices, LANES), f32),
        dma((chunks,)),
        dma((chunks,)),
        dma((chunks, others)),
        dma((chunks, others)),
        dma((chunks, others)),
        dma((chunks, others)),
        dma((half, chunks)),
        dma((half, chunks)),
    ]
    if mode != "first":
        scratch += [
            pltpu.VMEM((2, 2, 8, LANES), f32),
            pltpu.VMEM((n - 1, 2, 8, LANES), f32),
            pltpu.VMEM((max(slabs - 1, 1), 2, 8, LANES), f32),
            dma((n - 1,)),
            dma((n - 1,)),
            dma((max(slabs - 1, 1),)),
            dma((max(slabs - 1, 1),)),
        ]
    if mode == "last":
        scratch += [dma((2,)), dma((2,))]
    inputs = [part.reshape(half, 2, pieces, slices, LANES), weights, *extra]
    return pl.pallas_call(
        functools.partial(exchange_kernel, mode, n, slabs, chunks),
        out_shape=outs,
        in_specs=[VMEM] * len(inputs),
        out_specs=[VMEM] * len(outs),
        scratch_shapes=scratch,
        compiler_params=pltpu.CompilerParams(collective_id=ident, has_side_effects=True),
        name="exchange_" + mode,
    )(*inputs)


def shards(n, slabs, volume, measured, weights, footprints, foot_pixel, foot_strip):
    slices = volume.shape[0]
    blocks = volume.shape[1] // LANES
    count, rows, _ = footprints.shape
    slots = LANES // rows
    groups = STRIPS // slots
    shape = jax.ShapeDtypeStruct
    part_shape = shape((groups, slices, LANES), f32)
    grad_shape = shape((blocks, slices, LANES), f32)
    v3 = pltpu.VMEM((blocks, slices, 3 * LANES), bf16)

    def local(body, name, outs, scratch, *inputs):
        return pl.pallas_call(
            body,
            out_shape=outs,
            in_specs=[SMEM, SMEM] + [VMEM] * len(inputs),
            out_specs=[VMEM] * len(outs),
            scratch_shapes=scratch,
            name=name,
        )(foot_pixel, foot_strip, *inputs)

    fs, part = local(
        first_kernel,
        "project_first",
        [shape((count // slots, LANES, 2 * LANES), bf16), part_shape],
        [v3],
        volume,
        footprints.reshape(count // slots, LANES, LANES),
    )
    start, wr = exchange("first", part, weights, [measured], n, slabs, 1)
    first, part, square = local(
        middle_kernel,
        "gradient_first",
        [grad_shape, part_shape, shape((8, LANES), f32)],
        [v3],
        fs,
        wr.reshape(groups, slices, LANES),
    )
    projected, wp, sums = exchange("middle", part, weights, [square], n, slabs, 2)
    halo_shape = shape((2, 2, PASSES, blocks, LANES), f32)
    grad, part, square, current, halo = local(
        last_kernel,
        "gradient_second",
        [grad_shape, part_shape, shape((8, LANES), f32), grad_shape, halo_shape],
        [v3],
        fs,
        wp.reshape(groups, slices, LANES),
        first,
        volume,
        sums,
    )
    later, last_sums, halo_in = exchange("last", part, weights, [square, halo], n, slabs, 3)
    return pl.pallas_call(
        finish_kernel,
        out_shape=[shape(volume.shape, f32), shape(measured.shape, f32)],
        in_specs=[VMEM] * 8,
        out_specs=[VMEM] * 2,
        scratch_shapes=[pltpu.VMEM((blocks, slices + 16, LANES), f32)],
        name="smooth",
    )(current, grad, halo_in, last_sums, sums, start, projected, later)


def solution(mesh):
    return jax.shard_map(
        functools.partial(shards, mesh.shape["tile"], mesh.shape["slab"]),
        mesh=mesh,
        in_specs=(
            P("slab", "tile"),
            P("slab", "tile"),
            P("slab", "tile"),
            P("tile", None, None),
            P("tile"),
            P("tile"),
        ),
        out_specs=(P("slab", "tile"), P("slab", "tile")),
        check_vma=False,
    )
```

```python
import functools

import jax
import jax.numpy as jnp
from jax import lax
from jax.experimental import pallas as pl
from jax.experimental.pallas import tpu as pltpu
from jax.sharding import PartitionSpec as P

STRIPS = 256
PASSES = 3
LANES = 128
UNROLL = 16
MOST_CHUNKS = 4

huber_width = 0.5
smooth_rate = 0.2
MESH = pl.DeviceIdType.MESH
VMEM = pl.BlockSpec(memory_space=pltpu.VMEM)
SMEM = pl.BlockSpec(memory_space=pltpu.SMEM)
f32 = jnp.float32
bf16 = jnp.bfloat16


def halves(x):
    high = x.astype(bf16)
    return high, (x - high.astype(f32)).astype(bf16)


def triple(x):
    high, low = halves(x)
    return jnp.concatenate([high, low, high], axis=1)


def project(v3, fs, pix, strip, part):
    slices = v3.shape[1]
    slots = pix.shape[0] // fs.shape[0]
    rows = LANES // slots
    slot_of = lax.broadcasted_iota(jnp.int32, (slices, LANES), 1) // rows
    part[...] = jnp.zeros_like(part)

    def step(i, carry):
        found = []
        for u in range(UNROLL):
            t = i * UNROLL + u
            pair = fs[t]
            high, low = pair[:, :LANES], pair[:, LANES:]
            right = jnp.concatenate([high, high, low], axis=1)
            left = jnp.concatenate([v3[pix[t * slots + k]] for k in range(slots)], axis=0)
            out = lax.dot_general(
                left, right, (((1,), (1,)), ((), ())), preferred_element_type=f32
            )
            for k in range(slots):
                q = strip[t * slots + k]
                own = q % slots
                turned = pltpu.roll(
                    out[k * slices : (k + 1) * slices], ((own - k + slots) % slots) * rows, 1
                )
                found.append((q // slots, jnp.where(slot_of == own, turned, 0.0)))
        for g, out in found:
            part[g] += out
        return carry

    lax.fori_loop(0, fs.shape[0] // UNROLL, step, 0)


def back(wr, fs, pix, strip, grad):
    slices = wr.shape[1]
    slots = pix.shape[0] // fs.shape[0]
    rows = LANES // slots
    slot_of = lax.broadcasted_iota(jnp.int32, (slices, LANES), 1) // rows
    grad[...] = jnp.zeros_like(grad)

    def step(i, carry):
        found = []
        for u in range(UNROLL):
            t = i * UNROLL + u
            pair = fs[t]
            high, low = pair[:, :LANES], pair[:, LANES:]
            right = jnp.concatenate([high, high, low], axis=0)
            left = []
            for k in range(slots):
                q = strip[t * slots + k]
                turned = pltpu.roll(
                    wr[q // slots], ((k - q % slots + slots) % slots) * rows, 1
                )
                left.append(triple(jnp.where(slot_of == k, turned, 0.0)))
            out = lax.dot_general(
                jnp.concatenate(left, axis=0),
                right,
                (((1,), (0,)), ((), ())),
                preferred_element_type=f32,
            )
            for k in range(slots):
                found.append((pix[t * slots + k], out[k * slices : (k + 1) * slices]))
        for p, out in found:
            grad[p] += out
        return carry

    lax.fori_loop(0, fs.shape[0] // UNROLL, step, 0)


def first_kernel(pix, strip, volume, feet, fs, part, v3):
    for p in range(v3.shape[0]):
        v3[p] = triple(volume[:, p * LANES : (p + 1) * LANES])

    def split(i, carry):
        for u in range(UNROLL):
            t = i * UNROLL + u
            fs[t] = jnp.concatenate(halves(feet[t]), axis=1)
        return carry

    lax.fori_loop(0, feet.shape[0] // UNROLL, split, 0)
    project(v3, fs, pix, strip, part)


def fold8(x):
    return jnp.sum(x.reshape(x.shape[0] // 8, 8, LANES), axis=0)


def middle_kernel(pix, strip, fs, wr, grad, part, square, v3):
    back(wr, fs, pix, strip, grad)
    total = jnp.zeros((8, LANES), f32)
    for p in range(v3.shape[0]):
        value = grad[p]
        v3[p] = triple(value)
        total += fold8(value * value)
    square[...] = total
    project(v3, fs, pix, strip, part)


def last_kernel(pix, strip, fs, wr, first, volume, sums, grad, part, square, current, halo, v3):
    back(wr, fs, pix, strip, grad)
    rate = jnp.sum(sums[0]) / jnp.sum(sums[1])
    slices = grad.shape[1]
    total = jnp.zeros((8, LANES), f32)
    for p in range(v3.shape[0]):
        value = first[p] - rate * grad[p]
        now = volume[:, p * LANES : (p + 1) * LANES] - rate * first[p]
        grad[p] = value
        current[p] = now
        v3[p] = triple(value)
        total += fold8(value * value)
    square[...] = total
    for which, source in enumerate((current, grad)):
        for row in range(PASSES):
            halo[0, which, row] = source[:, slices - PASSES + row, :]
            halo[1, which, row] = source[:, row, :]
    project(v3, fs, pix, strip, part)


def finish_kernel(current, grad, halo, sums, rate_sums, start, projected, later, smoothed, residual, ext):
    rate0 = jnp.sum(rate_sums[0]) / jnp.sum(rate_sums[1])
    rate1 = jnp.sum(sums[0]) / jnp.sum(sums[1])
    count, slices, _ = current.shape
    for g in range(start.shape[0]):
        residual[:, g * LANES : (g + 1) * LANES] = (
            start[g] - rate0 * projected[g] - rate1 * later[g]
        )
    tall = slices + 16
    first_row = lax.axis_index("slab") * slices - 8
    total_rows = slices * lax.axis_size("slab")
    row = first_row + lax.broadcasted_iota(jnp.int32, (tall, LANES), 0)
    linked = (row >= 0) & (row + 1 < total_rows)
    for p in range(count):
        ext[p, 0:8] = jnp.zeros((8, LANES), f32)
        ext[p, 8 : 8 + slices] = current[p] - rate1 * grad[p]
        ext[p, 8 + slices :] = jnp.zeros((8, LANES), f32)
    for i in range(PASSES):
        ext[:, 8 - PASSES + i, :] = halo[0, 0, i] - rate1 * halo[0, 1, i]
        ext[:, 8 + slices + i, :] = halo[1, 0, i] - rate1 * halo[1, 1, i]
    for p in range(count):
        value = ext[p]
        for number in range(PASSES):
            differ = jnp.clip(pltpu.roll(value, tall - 1, 0) - value, -huber_width, huber_width)
            clipped = jnp.where(linked, differ, 0.0)
            value = value + smooth_rate * (clipped - pltpu.roll(clipped, 1, 0))
        smoothed[:, p * LANES : (p + 1) * LANES] = value[8 : 8 + slices]


def exchange_kernel(mode, n, slabs, chunks, *refs):
    refs = list(refs)
    part = refs.pop(0)
    weights = refs.pop(0)
    measured = refs.pop(0) if mode == "first" else None
    square = refs.pop(0) if mode != "first" else None
    halo = refs.pop(0) if mode == "last" else None
    own = refs.pop(0)
    gathered = refs.pop(0) if mode != "last" else None
    sums = refs.pop(0) if mode != "first" else None
    halo_in = refs.pop(0) if mode == "last" else None
    near, chip_sum, far, near_s, near_r, far_s, far_r, ag_s, ag_r, sib_s, sib_r = refs[:11]
    refs = refs[11:]
    if mode != "first":
        mine, tile_in, slab_in, t_s, t_r, b_s, b_r = refs[:7]
        refs = refs[7:]
    if mode == "last":
        h_s, h_r = refs

    half = n // 2
    pieces = part.shape[2]
    size = pieces // chunks
    me = lax.axis_index("tile")
    slab = lax.axis_index("slab")
    par = lax.rem(me, 2)
    row = me // 2
    sibling = me + 1 - 2 * par
    started = []

    def at(tile):
        return {"tile": tile}

    def along(other):
        return {"slab": other}

    def peer(d):
        return lax.rem(row + d, half) * 2 + par

    def send(src, dst, s, r, where):
        copy = pltpu.make_async_remote_copy(
            src_ref=src, dst_ref=dst, send_sem=s, recv_sem=r, device_id=where, device_id_type=MESH
        )
        copy.start()
        started.append(copy)
        return copy

    barrier = pltpu.get_barrier_semaphore()
    greeted = 0
    if mode == "first":
        tiles = [sibling] + [peer(d) for d in range(1, half)]
    else:
        tiles = [lax.rem(me + d, n) for d in range(1, n)]
    for tile in tiles:
        pl.semaphore_signal(barrier, inc=1, device_id=at(tile), device_id_type=MESH)
        greeted += 1
    if mode != "first":
        for d in range(1, slabs):
            pl.semaphore_signal(
                barrier, inc=1, device_id=along(lax.rem(slab + d, slabs)), device_id_type=MESH
            )
            greeted += 1
    pl.semaphore_wait(barrier, greeted)

    spans = [pl.ds(c * size, size) for c in range(chunks)]
    first_hop = [
        send(part.at[:, 1 - par, span], near.at[:, span], near_s.at[c], near_r.at[c], at(sibling))
        for c, span in enumerate(spans)
    ]
    second_hop = []
    for c, span in enumerate(spans):
        first_hop[c].wait_recv()
        for g in range(c * size, (c + 1) * size):
            for o in range(half):
                chip_sum[o, g] = part[o, par, g] + near[o, g]
        second_hop.append(
            [
                send(
                    chip_sum.at[lax.rem(row + d, half), span],
                    far.at[d - 1, span],
                    far_s.at[c, d - 1],
                    far_r.at[c, d - 1],
                    at(peer(d)),
                )
                for d in range(1, half)
            ]
        )
    if mode == "last":
        up = send(halo.at[0], halo_in.at[0], h_s.at[0], h_r.at[0], along(lax.rem(slab + 1, slabs)))
        down = send(
            halo.at[1], halo_in.at[1], h_s.at[1], h_r.at[1], along(lax.rem(slab + slabs - 1, slabs))
        )
    curve = jnp.zeros((8, LANES), f32)
    across = []
    aside = []
    for c, span in enumerate(spans):
        for copy in second_hop[c]:
            copy.wait_recv()
        for g in range(c * size, (c + 1) * size):
            value = chip_sum[row, g]
            for d in range(1, half):
                value += far[d - 1, g]
            lanes = slice(g * LANES, (g + 1) * LANES)
            if mode == "first":
                value = value - measured[:, lanes]
            weighted = weights[:, lanes] * value
            own[g] = value
            if mode != "first":
                curve += fold8(weighted * value)
            if mode != "last":
                gathered[row, par, g] = weighted
        if mode != "last":
            spot = gathered.at[row, par, span]
            across.append(
                [
                    send(spot, spot, ag_s.at[c, d - 1], ag_r.at[c, d - 1], at(peer(d)))
                    for d in range(1, half)
                ]
            )
            aside.append(send(spot, spot, sib_s.at[0, c], sib_r.at[0, c], at(sibling)))
    if mode != "first":
        mine[0, 0] = square[...]
        mine[0, 1] = curve
        tile_copies = [
            send(
                mine.at[0],
                tile_in.at[d - 1],
                t_s.at[d - 1],
                t_r.at[d - 1],
                at(lax.rem(me + d, n)),
            )
            for d in range(1, n)
        ]
    if mode != "last":
        for c, span in enumerate(spans):
            for d in range(1, half):
                across[c][d - 1].wait_recv()
                spot = gathered.at[lax.rem(row + half - d, half), par, span]
                aside.append(send(spot, spot, sib_s.at[d, c], sib_r.at[d, c], at(sibling)))
    if mode != "first":
        total = mine[0]
        for d in range(1, n):
            tile_copies[d - 1].wait_recv()
            total += tile_in[d - 1]
        mine[1] = total
        slab_copies = [
            send(
                mine.at[1],
                slab_in.at[d - 1],
                b_s.at[d - 1],
                b_r.at[d - 1],
                along(lax.rem(slab + d, slabs)),
            )
            for d in range(1, slabs)
        ]
        for d in range(1, slabs):
            slab_copies[d - 1].wait_recv()
            total += slab_in[d - 1]
        sums[...] = total
    for copy in aside:
        copy.wait_recv()
    if mode == "last":
        up.wait_recv()
        down.wait_recv()
    for copy in started:
        copy.wait_send()


def exchange(mode, part, weights, extra, n, slabs, ident):
    groups, slices, _ = part.shape
    half, pieces = n // 2, groups // n
    chunks = max(c for c in range(1, MOST_CHUNKS + 1) if pieces % c == 0)
    shape = jax.ShapeDtypeStruct
    outs = [shape((pieces, slices, LANES), f32)]
    if mode != "last":
        outs.append(shape((half, 2, pieces, slices, LANES), f32))
    if mode != "first":
        outs.append(shape((2, 8, LANES), f32))
    if mode == "last":
        outs.append(shape(extra[1].shape, f32))
    dma = pltpu.SemaphoreType.DMA
    others = max(half - 1, 1)
    scratch = [
        pltpu.VMEM((half, pieces, slices, LANES), f32),
        pltpu.VMEM((half, pieces, slices, LANES), f32),
        pltpu.VMEM((others, pieces, slices, LANES), f32),
        dma((chunks,)),
        dma((chunks,)),
        dma((chunks, others)),
        dma((chunks, others)),
        dma((chunks, others)),
        dma((chunks, others)),
        dma((half, chunks)),
        dma((half, chunks)),
    ]
    if mode != "first":
        scratch += [
            pltpu.VMEM((2, 2, 8, LANES), f32),
            pltpu.VMEM((n - 1, 2, 8, LANES), f32),
            pltpu.VMEM((max(slabs - 1, 1), 2, 8, LANES), f32),
            dma((n - 1,)),
            dma((n - 1,)),
            dma((max(slabs - 1, 1),)),
            dma((max(slabs - 1, 1),)),
        ]
    if mode == "last":
        scratch += [dma((2,)), dma((2,))]
    inputs = [part.reshape(half, 2, pieces, slices, LANES), weights, *extra]
    return pl.pallas_call(
        functools.partial(exchange_kernel, mode, n, slabs, chunks),
        out_shape=outs,
        in_specs=[VMEM] * len(inputs),
        out_specs=[VMEM] * len(outs),
        scratch_shapes=scratch,
        compiler_params=pltpu.CompilerParams(collective_id=ident, has_side_effects=True),
        name="exchange_" + mode,
    )(*inputs)


def shards(n, slabs, volume, measured, weights, footprints, foot_pixel, foot_strip):
    slices = volume.shape[0]
    blocks = volume.shape[1] // LANES
    count, rows, _ = footprints.shape
    slots = LANES // rows
    groups = STRIPS // slots
    shape = jax.ShapeDtypeStruct
    part_shape = shape((groups, slices, LANES), f32)
    grad_shape = shape((blocks, slices, LANES), f32)
    v3 = pltpu.VMEM((blocks, slices, 3 * LANES), bf16)

    def local(body, name, outs, scratch, *inputs):
        return pl.pallas_call(
            body,
            out_shape=outs,
            in_specs=[SMEM, SMEM] + [VMEM] * len(inputs),
            out_specs=[VMEM] * len(outs),
            scratch_shapes=scratch,
            name=name,
        )(foot_pixel, foot_strip, *inputs)

    fs, part = local(
        first_kernel,
        "project_first",
        [shape((count // slots, LANES, 2 * LANES), bf16), part_shape],
        [v3],
        volume,
        footprints.reshape(count // slots, LANES, LANES),
    )
    start, wr = exchange("first", part, weights, [measured], n, slabs, 1)
    first, part, square = local(
        middle_kernel,
        "gradient_first",
        [grad_shape, part_shape, shape((8, LANES), f32)],
        [v3],
        fs,
        wr.reshape(groups, slices, LANES),
    )
    projected, wp, sums = exchange("middle", part, weights, [square], n, slabs, 2)
    halo_shape = shape((2, 2, PASSES, blocks, LANES), f32)
    grad, part, square, current, halo = local(
        last_kernel,
        "gradient_second",
        [grad_shape, part_shape, shape((8, LANES), f32), grad_shape, halo_shape],
        [v3],
        fs,
        wp.reshape(groups, slices, LANES),
        first,
        volume,
        sums,
    )
    later, last_sums, halo_in = exchange("last", part, weights, [square, halo], n, slabs, 3)
    return pl.pallas_call(
        finish_kernel,
        out_shape=[shape(volume.shape, f32), shape(measured.shape, f32)],
        in_specs=[VMEM] * 8,
        out_specs=[VMEM] * 2,
        scratch_shapes=[pltpu.VMEM((blocks, slices + 16, LANES), f32)],
        name="smooth",
    )(current, grad, halo_in, last_sums, sums, start, projected, later)


def solution(mesh):
    return jax.shard_map(
        functools.partial(shards, mesh.shape["tile"], mesh.shape["slab"]),
        mesh=mesh,
        in_specs=(
            P("slab", "tile"),
            P("slab", "tile"),
            P("slab", "tile"),
            P("tile", None, None),
            P("tile"),
            P("tile"),
        ),
        out_specs=(P("slab", "tile"), P("slab", "tile")),
        check_vma=False,
    )
```

```python
import functools

import jax
import jax.numpy as jnp
from jax import lax
from jax.experimental import pallas as pl
from jax.experimental.pallas import tpu as pltpu
from jax.sharding import PartitionSpec as P

STRIPS = 256
PASSES = 3
LANES = 128
UNROLL = 16
MOST_CHUNKS = 4

huber_width = 0.5
smooth_rate = 0.2
MESH = pl.DeviceIdType.MESH
VMEM = pl.BlockSpec(memory_space=pltpu.VMEM)
SMEM = pl.BlockSpec(memory_space=pltpu.SMEM)
f32 = jnp.float32
bf16 = jnp.bfloat16


def halves(x):
    high = x.astype(bf16)
    return high, (x - high.astype(f32)).astype(bf16)


def triple(x):
    high, low = halves(x)
    return jnp.concatenate([high, low, high], axis=1)


def project(v3, fs, pix, strip, part):
    slices = v3.shape[1]
    slots = pix.shape[0] // fs.shape[0]
    rows = LANES // slots
    slot_of = lax.broadcasted_iota(jnp.int32, (slices, LANES), 1) // rows
    part[...] = jnp.zeros_like(part)

    def step(i, carry):
        found = []
        for u in range(UNROLL):
            t = i * UNROLL + u
            pair = fs[t]
            high, low = pair[:, :LANES], pair[:, LANES:]
            right = jnp.concatenate([high, high, low], axis=1)
            left = jnp.concatenate([v3[pix[t * slots + k]] for k in range(slots)], axis=0)
            out = lax.dot_general(
                left, right, (((1,), (1,)), ((), ())), preferred_element_type=f32
            )
            for k in range(slots):
                q = strip[t * slots + k]
                own = lax.bitwise_and(q, slots - 1)
                turned = pltpu.roll(
                    out[k * slices : (k + 1) * slices],
                    lax.bitwise_and(own + (slots - k), slots - 1) * rows,
                    1,
                )
                found.append(
                    (
                        lax.shift_right_logical(q, slots.bit_length() - 1),
                        jnp.where(slot_of == own, turned, 0.0),
                    )
                )
        for g, out in found:
            part[g] += out
        return carry

    lax.fori_loop(0, fs.shape[0] // UNROLL, step, 0)


def back(wr, fs, pix, strip, grad):
    slices = wr.shape[1]
    slots = pix.shape[0] // fs.shape[0]
    rows = LANES // slots
    slot_of = lax.broadcasted_iota(jnp.int32, (slices, LANES), 1) // rows
    grad[...] = jnp.zeros_like(grad)

    def step(i, carry):
        found = []
        for u in range(UNROLL):
            t = i * UNROLL + u
            pair = fs[t]
            high, low = pair[:, :LANES], pair[:, LANES:]
            right = jnp.concatenate([high, high, low], axis=0)
            left = []
            for k in range(slots):
                q = strip[t * slots + k]
                turned = pltpu.roll(
                    wr[lax.shift_right_logical(q, slots.bit_length() - 1)],
                    lax.bitwise_and(k + slots - lax.bitwise_and(q, slots - 1), slots - 1) * rows,
                    1,
                )
                left.append(triple(jnp.where(slot_of == k, turned, 0.0)))
            out = lax.dot_general(
                jnp.concatenate(left, axis=0),
                right,
                (((1,), (0,)), ((), ())),
                preferred_element_type=f32,
            )
            for k in range(slots):
                found.append((pix[t * slots + k], out[k * slices : (k + 1) * slices]))
        for p, out in found:
            grad[p] += out
        return carry

    lax.fori_loop(0, fs.shape[0] // UNROLL, step, 0)


def first_kernel(pix, strip, volume, feet, fs, part, v3):
    for p in range(v3.shape[0]):
        v3[p] = triple(volume[:, p * LANES : (p + 1) * LANES])

    def split(i, carry):
        for u in range(UNROLL):
            t = i * UNROLL + u
            fs[t] = jnp.concatenate(halves(feet[t]), axis=1)
        return carry

    lax.fori_loop(0, feet.shape[0] // UNROLL, split, 0)
    project(v3, fs, pix, strip, part)


def fold8(x):
    return jnp.sum(x.reshape(x.shape[0] // 8, 8, LANES), axis=0)


def middle_kernel(pix, strip, fs, wr, grad, part, square, v3):
    back(wr, fs, pix, strip, grad)
    total = jnp.zeros((8, LANES), f32)
    for p in range(v3.shape[0]):
        value = grad[p]
        v3[p] = triple(value)
        total += fold8(value * value)
    square[...] = total
    project(v3, fs, pix, strip, part)


def last_kernel(pix, strip, fs, wr, first, volume, grad, part, halo, v3):
    back(wr, fs, pix, strip, grad)
    slices = grad.shape[1]
    blocks = v3.shape[0]
    for p in range(blocks):
        v3[p] = triple(grad[p])
    for row in range(PASSES):
        for side, spot in enumerate((slices - PASSES + row, row)):
            for p in range(blocks):
                halo[side, 0, row, p : p + 1] = volume[
                    spot : spot + 1, p * LANES : (p + 1) * LANES
                ]
            halo[side, 1, row] = first[:, spot, :]
            halo[side, 2, row] = grad[:, spot, :]
    project(v3, fs, pix, strip, part)


def finish_kernel(volume, first, turned, halo, sums, start, projected, later, smoothed, residual, ext):
    rate0 = jnp.sum(sums[0, 0]) / jnp.sum(sums[0, 1])
    rate1 = jnp.sum(sums[1, 0]) / jnp.sum(sums[1, 1])

    def stepped(image, one, two):
        return image - rate0 * one - rate1 * (one - rate0 * two)

    count, slices, _ = first.shape
    for g in range(start.shape[0]):
        residual[:, g * LANES : (g + 1) * LANES] = (
            start[g] - rate0 * projected[g] - rate1 * later[g]
        )
    tall = slices + 16
    first_row = lax.axis_index("slab") * slices - 8
    total_rows = slices * lax.axis_size("slab")
    row = first_row + lax.broadcasted_iota(jnp.int32, (tall, LANES), 0)
    linked = (row >= 0) & (row + 1 < total_rows)
    for p in range(count):
        ext[p, 0:8] = jnp.zeros((8, LANES), f32)
        ext[p, 8 : 8 + slices] = stepped(
            volume[:, p * LANES : (p + 1) * LANES], first[p], turned[p]
        )
        ext[p, 8 + slices :] = jnp.zeros((8, LANES), f32)
    for i in range(PASSES):
        ext[:, 8 - PASSES + i, :] = stepped(halo[0, 0, i], halo[0, 1, i], halo[0, 2, i])
        ext[:, 8 + slices + i, :] = stepped(halo[1, 0, i], halo[1, 1, i], halo[1, 2, i])
    for p in range(count):
        value = ext[p]
        for number in range(PASSES):
            differ = jnp.clip(pltpu.roll(value, tall - 1, 0) - value, -huber_width, huber_width)
            clipped = jnp.where(linked, differ, 0.0)
            value = value + smooth_rate * (clipped - pltpu.roll(clipped, 1, 0))
        smoothed[:, p * LANES : (p + 1) * LANES] = value[8 : 8 + slices]


def exchange_kernel(mode, n, slabs, chunks, *refs):
    refs = list(refs)
    part = refs.pop(0)
    weights = refs.pop(0)
    measured = refs.pop(0) if mode == "first" else None
    if mode == "last":
        projected, square, first, turned, halo = refs[:5]
        refs = refs[5:]
    own = refs.pop(0)
    gathered = refs.pop(0) if mode != "last" else None
    sums = refs.pop(0) if mode == "last" else None
    halo_in = refs.pop(0) if mode == "last" else None
    near, chip_sum, far, near_s, near_r, far_s, far_r, ag_s, ag_r, sib_s, sib_r = refs[:11]
    refs = refs[11:]
    if mode == "last":
        mine, tile_in, slab_in, t_s, t_r, b_s, b_r, h_s, h_r = refs

    half = n // 2
    pieces = part.shape[2]
    size = pieces // chunks
    me = lax.axis_index("tile")
    slab = lax.axis_index("slab")
    par = lax.rem(me, 2)
    row = me // 2
    sibling = me + 1 - 2 * par
    started = []

    def at(tile):
        return {"tile": tile}

    def along(other):
        return {"slab": other}

    def peer(d):
        return lax.rem(row + d, half) * 2 + par

    def send(src, dst, s, r, where):
        copy = pltpu.make_async_remote_copy(
            src_ref=src, dst_ref=dst, send_sem=s, recv_sem=r, device_id=where, device_id_type=MESH
        )
        copy.start()
        started.append(copy)
        return copy

    barrier = pltpu.get_barrier_semaphore()
    greeted = 0
    if mode != "last":
        tiles = [sibling] + [peer(d) for d in range(1, half)]
    else:
        tiles = [lax.rem(me + d, n) for d in range(1, n)]
    for tile in tiles:
        pl.semaphore_signal(barrier, inc=1, device_id=at(tile), device_id_type=MESH)
        greeted += 1
    if mode == "last":
        for d in range(1, slabs):
            pl.semaphore_signal(
                barrier, inc=1, device_id=along(lax.rem(slab + d, slabs)), device_id_type=MESH
            )
            greeted += 1
    pl.semaphore_wait(barrier, greeted)

    spans = [pl.ds(c * size, size) for c in range(chunks)]
    first_hop = [
        send(part.at[:, 1 - par, span], near.at[:, span], near_s.at[c], near_r.at[c], at(sibling))
        for c, span in enumerate(spans)
    ]
    def tile_round(k, top, bottom):
        mine[k, 0, 0] = top
        mine[k, 0, 1] = bottom
        return [
            send(
                mine.at[k, 0],
                tile_in.at[k, d - 1],
                t_s.at[k, d - 1],
                t_r.at[k, d - 1],
                at(lax.rem(me + d, n)),
            )
            for d in range(1, n)
        ]

    def slab_round(k, copies):
        total = mine[k, 0]
        for d in range(1, n):
            copies[d - 1].wait_recv()
            total += tile_in[k, d - 1]
        mine[k, 1] = total
        return [
            send(
                mine.at[k, 1],
                slab_in.at[k, d - 1],
                b_s.at[k, d - 1],
                b_r.at[k, d - 1],
                along(lax.rem(slab + d, slabs)),
            )
            for d in range(1, slabs)
        ]

    def end_round(k, copies):
        total = mine[k, 1]
        for d in range(1, slabs):
            copies[d - 1].wait_recv()
            total += slab_in[k, d - 1]
        sums[k] = total
        return total

    if mode == "last":
        up = send(halo.at[0], halo_in.at[0], h_s.at[0], h_r.at[0], along(lax.rem(slab + 1, slabs)))
        down = send(
            halo.at[1], halo_in.at[1], h_s.at[1], h_r.at[1], along(lax.rem(slab + slabs - 1, slabs))
        )
        curve = jnp.zeros((8, LANES), f32)
        for g in range(pieces):
            value = projected[g]
            curve += fold8(weights[:, g * LANES : (g + 1) * LANES] * value * value)
        round0 = tile_round(0, square[...], curve)
    second_hop = []
    for c, span in enumerate(spans):
        first_hop[c].wait_recv()
        for g in range(c * size, (c + 1) * size):
            for o in range(half):
                chip_sum[o, g] = part[o, par, g] + near[o, g]
        second_hop.append(
            [
                send(
                    chip_sum.at[lax.rem(row + d, half), span],
                    far.at[d - 1, span],
                    far_s.at[c, d - 1],
                    far_r.at[c, d - 1],
                    at(peer(d)),
                )
                for d in range(1, half)
            ]
        )
    if mode == "last":
        total = end_round(0, slab_round(0, round0))
        rate = jnp.sum(total[0]) / jnp.sum(total[1])

        def add_square(p, carry):
            value = first[p] - rate * turned[p]
            return carry + fold8(value * value)

        squares = lax.fori_loop(0, first.shape[0], add_square, jnp.zeros((8, LANES), f32))
        curve = jnp.zeros((8, LANES), f32)
    across = []
    aside = []
    for c, span in enumerate(spans):
        for copy in second_hop[c]:
            copy.wait_recv()
        for g in range(c * size, (c + 1) * size):
            value = chip_sum[row, g]
            for d in range(1, half):
                value += far[d - 1, g]
            lanes = slice(g * LANES, (g + 1) * LANES)
            if mode == "first":
                value = value - measured[:, lanes]
            if mode == "last":
                value = projected[g] - rate * value
            weighted = weights[:, lanes] * value
            own[g] = value
            if mode == "last":
                curve += fold8(weighted * value)
            if mode != "last":
                gathered[row, par, g] = weighted
        if mode != "last":
            spot = gathered.at[row, par, span]
            across.append(
                [
                    send(spot, spot, ag_s.at[c, d - 1], ag_r.at[c, d - 1], at(peer(d)))
                    for d in range(1, half)
                ]
            )
            aside.append(send(spot, spot, sib_s.at[0, c], sib_r.at[0, c], at(sibling)))
    if mode != "last":
        for c, span in enumerate(spans):
            for d in range(1, half):
                across[c][d - 1].wait_recv()
                spot = gathered.at[lax.rem(row + half - d, half), par, span]
                aside.append(send(spot, spot, sib_s.at[d, c], sib_r.at[d, c], at(sibling)))
    if mode == "last":
        end_round(1, slab_round(1, tile_round(1, squares, curve)))
    for copy in aside:
        copy.wait_recv()
    if mode == "last":
        up.wait_recv()
        down.wait_recv()
    for copy in started:
        copy.wait_send()


def exchange(mode, part, weights, extra, n, slabs, ident):
    groups, slices, _ = part.shape
    half, pieces = n // 2, groups // n
    chunks = max(c for c in range(1, MOST_CHUNKS + 1) if pieces % c == 0)
    shape = jax.ShapeDtypeStruct
    outs = [shape((pieces, slices, LANES), f32)]
    if mode != "last":
        outs.append(shape((half, 2, pieces, slices, LANES), f32))
    if mode == "last":
        outs.append(shape((2, 2, 8, LANES), f32))
        outs.append(shape(extra[-1].shape, f32))
    dma = pltpu.SemaphoreType.DMA
    others = max(half - 1, 1)
    scratch = [
        pltpu.VMEM((half, pieces, slices, LANES), f32),
        pltpu.VMEM((half, pieces, slices, LANES), f32),
        pltpu.VMEM((others, pieces, slices, LANES), f32),
        dma((chunks,)),
        dma((chunks,)),
        dma((chunks, others)),
        dma((chunks, others)),
        dma((chunks, others)),
        dma((chunks, others)),
        dma((half, chunks)),
        dma((half, chunks)),
    ]
    if mode == "last":
        around = max(slabs - 1, 1)
        scratch += [
            pltpu.VMEM((2, 2, 2, 8, LANES), f32),
            pltpu.VMEM((2, n - 1, 2, 8, LANES), f32),
            pltpu.VMEM((2, around, 2, 8, LANES), f32),
            dma((2, n - 1)),
            dma((2, n - 1)),
            dma((2, around)),
            dma((2, around)),
            dma((2,)),
            dma((2,)),
        ]
    inputs = [part.reshape(half, 2, pieces, slices, LANES), weights, *extra]
    return pl.pallas_call(
        functools.partial(exchange_kernel, mode, n, slabs, chunks),
        out_shape=outs,
        in_specs=[VMEM] * len(inputs),
        out_specs=[VMEM] * len(outs),
        scratch_shapes=scratch,
        compiler_params=pltpu.CompilerParams(collective_id=ident, has_side_effects=True),
        name="exchange_" + mode,
    )(*inputs)


def shards(n, slabs, volume, measured, weights, footprints, foot_pixel, foot_strip):
    slices = volume.shape[0]
    blocks = volume.shape[1] // LANES
    count, rows, _ = footprints.shape
    slots = LANES // rows
    groups = STRIPS // slots
    shape = jax.ShapeDtypeStruct
    part_shape = shape((groups, slices, LANES), f32)
    grad_shape = shape((blocks, slices, LANES), f32)
    v3 = pltpu.VMEM((blocks, slices, 3 * LANES), bf16)

    def local(body, name, outs, scratch, *inputs):
        return pl.pallas_call(
            body,
            out_shape=outs,
            in_specs=[SMEM, SMEM] + [VMEM] * len(inputs),
            out_specs=[VMEM] * len(outs),
            scratch_shapes=scratch,
            name=name,
        )(foot_pixel, foot_strip, *inputs)

    fs, part = local(
        first_kernel,
        "project_first",
        [shape((count // slots, LANES, 2 * LANES), bf16), part_shape],
        [v3],
        volume,
        footprints.reshape(count // slots, LANES, LANES),
    )
    start, wr = exchange("first", part, weights, [measured], n, slabs, 1)
    first, part, square = local(
        middle_kernel,
        "gradient_first",
        [grad_shape, part_shape, shape((8, LANES), f32)],
        [v3],
        fs,
        wr.reshape(groups, slices, LANES),
    )
    projected, wp = exchange("middle", part, weights, [], n, slabs, 2)
    halo_shape = shape((2, 3, PASSES, blocks, LANES), f32)
    turned, part, halo = local(
        last_kernel,
        "gradient_second",
        [grad_shape, part_shape, halo_shape],
        [v3],
        fs,
        wp.reshape(groups, slices, LANES),
        first,
        volume,
    )
    later, sums, halo_in = exchange(
        "last", part, weights, [projected, square, first, turned, halo], n, slabs, 3
    )
    return pl.pallas_call(
        finish_kernel,
        out_shape=[shape(volume.shape, f32), shape(measured.shape, f32)],
        in_specs=[VMEM] * 8,
        out_specs=[VMEM] * 2,
        scratch_shapes=[pltpu.VMEM((blocks, slices + 16, LANES), f32)],
        name="smooth",
    )(volume, first, turned, halo_in, sums, start, projected, later)


def solution(mesh):
    return jax.shard_map(
        functools.partial(shards, mesh.shape["tile"], mesh.shape["slab"]),
        mesh=mesh,
        in_specs=(
            P("slab", "tile"),
            P("slab", "tile"),
            P("slab", "tile"),
            P("tile", None, None),
            P("tile"),
            P("tile"),
        ),
        out_specs=(P("slab", "tile"), P("slab", "tile")),
        check_vma=False,
    )
```

```python
import functools

import jax
import jax.numpy as jnp
from jax import lax
from jax.experimental import pallas as pl
from jax.experimental.pallas import tpu as pltpu
from jax.sharding import PartitionSpec as P

STRIPS = 256
PASSES = 3
LANES = 128
UNROLL = 32
STAGE = 16
MOST_CHUNKS = 8

huber_width = 0.5
smooth_rate = 0.2
MESH = pl.DeviceIdType.MESH
VMEM = pl.BlockSpec(memory_space=pltpu.VMEM)
SMEM = pl.BlockSpec(memory_space=pltpu.SMEM)
f32 = jnp.float32
bf16 = jnp.bfloat16


def halves(x):
    high = x.astype(bf16)
    return high, (x - high.astype(f32)).astype(bf16)


def triple(x):
    high, low = halves(x)
    return jnp.concatenate([high, low, high], axis=1)


def project(v3, fs, pix, strip, part, stage=0, stages=1):
    slices = v3.shape[1]
    slots = pix.shape[0] // (fs.shape[0] * stages)
    base = stage * fs.shape[0]
    rows = LANES // slots
    slot_of = lax.broadcasted_iota(jnp.int32, (slices, LANES), 1) // rows

    unroll = min(UNROLL, fs.shape[0])

    def step(i, carry):
        found = []
        for u in range(unroll):
            t = i * unroll + u
            pair = fs[t]
            high, low = pair[:, :LANES], pair[:, LANES:]
            right = jnp.concatenate([high, high, low], axis=1)
            left = jnp.concatenate([v3[pix[(base + t) * slots + k]] for k in range(slots)], axis=0)
            out = lax.dot_general(
                left, right, (((1,), (1,)), ((), ())), preferred_element_type=f32
            )
            for k in range(slots):
                q = strip[(base + t) * slots + k]
                own = lax.bitwise_and(q, slots - 1)
                turned = pltpu.roll(
                    out[k * slices : (k + 1) * slices],
                    lax.bitwise_and(own + (slots - k), slots - 1) * rows,
                    1,
                )
                found.append(
                    (
                        lax.shift_right_logical(q, slots.bit_length() - 1),
                        jnp.where(slot_of == own, turned, 0.0),
                    )
                )
        for g, out in found:
            part[g] += out
        return carry

    lax.fori_loop(0, fs.shape[0] // unroll, step, 0)


def back(wr, fs, pix, strip, grad):
    slices = wr.shape[1]
    slots = pix.shape[0] // fs.shape[0]
    rows = LANES // slots
    slot_of = lax.broadcasted_iota(jnp.int32, (slices, LANES), 1) // rows
    grad[...] = jnp.zeros_like(grad)

    unroll = min(UNROLL, fs.shape[0])

    def step(i, carry):
        found = []
        for u in range(unroll):
            t = i * unroll + u
            pair = fs[t]
            high, low = pair[:, :LANES], pair[:, LANES:]
            right = jnp.concatenate([high, high, low], axis=0)
            left = []
            for k in range(slots):
                q = strip[t * slots + k]
                turned = pltpu.roll(
                    wr[lax.shift_right_logical(q, slots.bit_length() - 1)],
                    lax.bitwise_and(k + slots - lax.bitwise_and(q, slots - 1), slots - 1) * rows,
                    1,
                )
                left.append(triple(jnp.where(slot_of == k, turned, 0.0)))
            out = lax.dot_general(
                jnp.concatenate(left, axis=0),
                right,
                (((1,), (0,)), ((), ())),
                preferred_element_type=f32,
            )
            for k in range(slots):
                found.append((pix[t * slots + k], out[k * slices : (k + 1) * slices]))
        for p, out in found:
            grad[p] += out
        return carry

    lax.fori_loop(0, fs.shape[0] // unroll, step, 0)


def first_kernel(stages, pix, strip, volume, feet, fs, part, v3):
    stage = pl.program_id(0)

    @pl.when(stage == 0)
    def _():
        part[...] = jnp.zeros_like(part)
        for p in range(v3.shape[0]):
            v3[p] = triple(volume[:, p * LANES : (p + 1) * LANES])

    for t in range(feet.shape[0]):
        fs[t] = jnp.concatenate(halves(feet[t]), axis=1)
    project(v3, fs, pix, strip, part, stage, stages)


def fold8(x):
    return jnp.sum(x.reshape(x.shape[0] // 8, 8, LANES), axis=0)


def middle_kernel(pix, strip, fs, wr, grad, part, square, v3):
    back(wr, fs, pix, strip, grad)
    total = jnp.zeros((8, LANES), f32)
    for p in range(v3.shape[0]):
        value = grad[p]
        v3[p] = triple(value)
        total += fold8(value * value)
    square[...] = total
    part[...] = jnp.zeros_like(part)
    project(v3, fs, pix, strip, part)


def last_kernel(pix, strip, fs, wr, first, volume, grad, part, halo, v3):
    back(wr, fs, pix, strip, grad)
    slices = grad.shape[1]
    blocks = v3.shape[0]
    for p in range(blocks):
        v3[p] = triple(grad[p])
    for row in range(PASSES):
        for side, spot in enumerate((slices - PASSES + row, row)):
            for p in range(blocks):
                halo[side, 0, row, p : p + 1] = volume[
                    spot : spot + 1, p * LANES : (p + 1) * LANES
                ]
            halo[side, 1, row] = first[:, spot, :]
            halo[side, 2, row] = grad[:, spot, :]
    part[...] = jnp.zeros_like(part)
    project(v3, fs, pix, strip, part)


def finish_kernel(volume, first, turned, halo, sums, start, projected, later, smoothed, residual, ext):
    rate0 = jnp.sum(sums[0, 0]) / jnp.sum(sums[0, 1])
    rate1 = jnp.sum(sums[1, 0]) / jnp.sum(sums[1, 1])

    def stepped(image, one, two):
        return image - rate0 * one - rate1 * (one - rate0 * two)

    count, slices, _ = first.shape
    for g in range(start.shape[0]):
        residual[:, g * LANES : (g + 1) * LANES] = (
            start[g] - rate0 * projected[g] - rate1 * later[g]
        )
    tall = slices + 16
    first_row = lax.axis_index("slab") * slices - 8
    total_rows = slices * lax.axis_size("slab")
    row = first_row + lax.broadcasted_iota(jnp.int32, (tall, LANES), 0)
    linked = (row >= 0) & (row + 1 < total_rows)
    for p in range(count):
        ext[p, 0:8] = jnp.zeros((8, LANES), f32)
        ext[p, 8 : 8 + slices] = stepped(
            volume[:, p * LANES : (p + 1) * LANES], first[p], turned[p]
        )
        ext[p, 8 + slices :] = jnp.zeros((8, LANES), f32)
    for i in range(PASSES):
        ext[:, 8 - PASSES + i, :] = stepped(halo[0, 0, i], halo[0, 1, i], halo[0, 2, i])
        ext[:, 8 + slices + i, :] = stepped(halo[1, 0, i], halo[1, 1, i], halo[1, 2, i])
    for p in range(count):
        value = ext[p]
        for number in range(PASSES):
            differ = jnp.clip(pltpu.roll(value, tall - 1, 0) - value, -huber_width, huber_width)
            clipped = jnp.where(linked, differ, 0.0)
            value = value + smooth_rate * (clipped - pltpu.roll(clipped, 1, 0))
        smoothed[:, p * LANES : (p + 1) * LANES] = value[8 : 8 + slices]


def exchange_kernel(mode, n, slabs, chunks, *refs):
    refs = list(refs)
    part = refs.pop(0)
    weights = refs.pop(0)
    measured = refs.pop(0) if mode == "first" else None
    if mode == "last":
        projected, square, first, turned, halo = refs[:5]
        refs = refs[5:]
    own = refs.pop(0)
    gathered = refs.pop(0) if mode != "last" else None
    sums = refs.pop(0) if mode == "last" else None
    halo_in = refs.pop(0) if mode == "last" else None
    near, chip_sum, far, near_s, near_r, far_s, far_r, ag_s, ag_r, sib_s, sib_r = refs[:11]
    refs = refs[11:]
    if mode == "last":
        mine, tile_in, slab_in, t_s, t_r, b_s, b_r, h_s, h_r = refs

    half = n // 2
    pieces = part.shape[2]
    size = pieces // chunks
    me = lax.axis_index("tile")
    slab = lax.axis_index("slab")
    par = lax.rem(me, 2)
    row = me // 2
    sibling = me + 1 - 2 * par
    started = []

    def at(tile):
        return {"tile": tile}

    def along(other):
        return {"slab": other}

    def peer(d):
        return lax.rem(row + d, half) * 2 + par

    def send(src, dst, s, r, where):
        copy = pltpu.make_async_remote_copy(
            src_ref=src, dst_ref=dst, send_sem=s, recv_sem=r, device_id=where, device_id_type=MESH
        )
        copy.start()
        started.append(copy)
        return copy

    barrier = pltpu.get_barrier_semaphore()
    greeted = 0
    if mode != "last":
        tiles = [sibling] + [peer(d) for d in range(1, half)]
    else:
        tiles = [lax.rem(me + d, n) for d in range(1, n)]
    for tile in tiles:
        pl.semaphore_signal(barrier, inc=1, device_id=at(tile), device_id_type=MESH)
        greeted += 1
    if mode == "last":
        for d in range(1, slabs):
            pl.semaphore_signal(
                barrier, inc=1, device_id=along(lax.rem(slab + d, slabs)), device_id_type=MESH
            )
            greeted += 1
    pl.semaphore_wait(barrier, greeted)

    spans = [pl.ds(c * size, size) for c in range(chunks)]
    first_hop = [
        send(part.at[:, 1 - par, span], near.at[:, span], near_s.at[c], near_r.at[c], at(sibling))
        for c, span in enumerate(spans)
    ]
    def tile_round(k, top, bottom):
        mine[k, 0, 0] = top
        mine[k, 0, 1] = bottom
        return [
            send(
                mine.at[k, 0],
                tile_in.at[k, d - 1],
                t_s.at[k, d - 1],
                t_r.at[k, d - 1],
                at(lax.rem(me + d, n)),
            )
            for d in range(1, n)
        ]

    def slab_round(k, copies):
        total = mine[k, 0]
        for d in range(1, n):
            copies[d - 1].wait_recv()
            total += tile_in[k, d - 1]
        mine[k, 1] = total
        return [
            send(
                mine.at[k, 1],
                slab_in.at[k, d - 1],
                b_s.at[k, d - 1],
                b_r.at[k, d - 1],
                along(lax.rem(slab + d, slabs)),
            )
            for d in range(1, slabs)
        ]

    def end_round(k, copies):
        total = mine[k, 1]
        for d in range(1, slabs):
            copies[d - 1].wait_recv()
            total += slab_in[k, d - 1]
        sums[k] = total
        return total

    if mode == "last":
        curve = jnp.zeros((8, LANES), f32)
        for g in range(pieces):
            value = projected[g]
            curve += fold8(weights[:, g * LANES : (g + 1) * LANES] * value * value)
        round0 = tile_round(0, square[...], curve)
    second_hop = []
    for c, span in enumerate(spans):
        first_hop[c].wait_recv()
        for g in range(c * size, (c + 1) * size):
            for o in range(half):
                chip_sum[o, g] = part[o, par, g] + near[o, g]
        second_hop.append(
            [
                send(
                    chip_sum.at[lax.rem(row + d, half), span],
                    far.at[d - 1, span],
                    far_s.at[c, d - 1],
                    far_r.at[c, d - 1],
                    at(peer(d)),
                )
                for d in range(1, half)
            ]
        )
    if mode == "last":
        round0 = slab_round(0, round0)
        up = send(halo.at[0], halo_in.at[0], h_s.at[0], h_r.at[0], along(lax.rem(slab + 1, slabs)))
        down = send(
            halo.at[1], halo_in.at[1], h_s.at[1], h_r.at[1], along(lax.rem(slab + slabs - 1, slabs))
        )
        total = end_round(0, round0)
        rate = jnp.sum(total[0]) / jnp.sum(total[1])

        def add_square(p, carry):
            value = first[p] - rate * turned[p]
            return carry + fold8(value * value)

        squares = lax.fori_loop(0, first.shape[0], add_square, jnp.zeros((8, LANES), f32))
        curve = jnp.zeros((8, LANES), f32)
    across = []
    aside = []
    for c, span in enumerate(spans):
        for copy in second_hop[c]:
            copy.wait_recv()
        for g in range(c * size, (c + 1) * size):
            value = chip_sum[row, g]
            for d in range(1, half):
                value += far[d - 1, g]
            lanes = slice(g * LANES, (g + 1) * LANES)
            if mode == "first":
                value = value - measured[:, lanes]
            if mode == "last":
                value = projected[g] - rate * value
            weighted = weights[:, lanes] * value
            own[g] = value
            if mode == "last":
                curve += fold8(weighted * value)
            if mode != "last":
                gathered[row, par, g] = weighted
        if mode != "last":
            spot = gathered.at[row, par, span]
            across.append(
                [
                    send(spot, spot, ag_s.at[c, d - 1], ag_r.at[c, d - 1], at(peer(d)))
                    for d in range(1, half)
                ]
            )
            aside.append(send(spot, spot, sib_s.at[0, c], sib_r.at[0, c], at(sibling)))
    if mode != "last":
        for c, span in enumerate(spans):
            for d in range(1, half):
                across[c][d - 1].wait_recv()
                spot = gathered.at[lax.rem(row + half - d, half), par, span]
                aside.append(send(spot, spot, sib_s.at[d, c], sib_r.at[d, c], at(sibling)))
    if mode == "last":
        end_round(1, slab_round(1, tile_round(1, squares, curve)))
    for copy in aside:
        copy.wait_recv()
    if mode == "last":
        up.wait_recv()
        down.wait_recv()
    for copy in started:
        copy.wait_send()


def exchange(mode, part, weights, extra, n, slabs, ident):
    groups, slices, _ = part.shape
    half, pieces = n // 2, groups // n
    chunks = max(c for c in range(1, MOST_CHUNKS + 1) if pieces % c == 0)
    shape = jax.ShapeDtypeStruct
    outs = [shape((pieces, slices, LANES), f32)]
    if mode != "last":
        outs.append(shape((half, 2, pieces, slices, LANES), f32))
    if mode == "last":
        outs.append(shape((2, 2, 8, LANES), f32))
        outs.append(shape(extra[-1].shape, f32))
    dma = pltpu.SemaphoreType.DMA
    others = max(half - 1, 1)
    scratch = [
        pltpu.VMEM((half, pieces, slices, LANES), f32),
        pltpu.VMEM((half, pieces, slices, LANES), f32),
        pltpu.VMEM((others, pieces, slices, LANES), f32),
        dma((chunks,)),
        dma((chunks,)),
        dma((chunks, others)),
        dma((chunks, others)),
        dma((chunks, others)),
        dma((chunks, others)),
        dma((half, chunks)),
        dma((half, chunks)),
    ]
    if mode == "last":
        around = max(slabs - 1, 1)
        scratch += [
            pltpu.VMEM((2, 2, 2, 8, LANES), f32),
            pltpu.VMEM((2, n - 1, 2, 8, LANES), f32),
            pltpu.VMEM((2, around, 2, 8, LANES), f32),
            dma((2, n - 1)),
            dma((2, n - 1)),
            dma((2, around)),
            dma((2, around)),
            dma((2,)),
            dma((2,)),
        ]
    inputs = [part.reshape(half, 2, pieces, slices, LANES), weights, *extra]
    return pl.pallas_call(
        functools.partial(exchange_kernel, mode, n, slabs, chunks),
        out_shape=outs,
        in_specs=[VMEM] * len(inputs),
        out_specs=[VMEM] * len(outs),
        scratch_shapes=scratch,
        compiler_params=pltpu.CompilerParams(collective_id=ident, has_side_effects=True),
        name="exchange_" + mode,
    )(*inputs)


def shards(n, slabs, volume, measured, weights, footprints, foot_pixel, foot_strip):
    slices = volume.shape[0]
    blocks = volume.shape[1] // LANES
    count, rows, _ = footprints.shape
    slots = LANES // rows
    groups = STRIPS // slots
    shape = jax.ShapeDtypeStruct
    part_shape = shape((groups, slices, LANES), f32)
    grad_shape = shape((blocks, slices, LANES), f32)
    v3 = pltpu.VMEM((blocks, slices, 3 * LANES), bf16)

    def local(body, name, outs, scratch, *inputs):
        return pl.pallas_call(
            body,
            out_shape=outs,
            in_specs=[SMEM, SMEM] + [VMEM] * len(inputs),
            out_specs=[VMEM] * len(outs),
            scratch_shapes=scratch,
            name=name,
        )(foot_pixel, foot_strip, *inputs)

    size = min(STAGE, count // slots)
    stages = count // slots // size
    fs, part = pl.pallas_call(
        functools.partial(first_kernel, stages),
        grid=(stages,),
        out_shape=[shape((count // slots, LANES, 2 * LANES), bf16), part_shape],
        in_specs=[
            SMEM,
            SMEM,
            pl.BlockSpec(volume.shape, lambda i: (0, 0)),
            pl.BlockSpec((size, LANES, LANES), lambda i: (i, 0, 0)),
        ],
        out_specs=[
            pl.BlockSpec((size, LANES, 2 * LANES), lambda i: (i, 0, 0)),
            pl.BlockSpec(part_shape.shape, lambda i: (0, 0, 0)),
        ],
        scratch_shapes=[v3],
        name="project_first",
    )(foot_pixel, foot_strip, volume, footprints.reshape(count // slots, LANES, LANES))
    start, wr = exchange("first", part, weights, [measured], n, slabs, 1)
    first, part, square = local(
        middle_kernel,
        "gradient_first",
        [grad_shape, part_shape, shape((8, LANES), f32)],
        [v3],
        fs,
        wr.reshape(groups, slices, LANES),
    )
    projected, wp = exchange("middle", part, weights, [], n, slabs, 2)
    halo_shape = shape((2, 3, PASSES, blocks, LANES), f32)
    turned, part, halo = local(
        last_kernel,
        "gradient_second",
        [grad_shape, part_shape, halo_shape],
        [v3],
        fs,
        wp.reshape(groups, slices, LANES),
        first,
        volume,
    )
    later, sums, halo_in = exchange(
        "last", part, weights, [projected, square, first, turned, halo], n, slabs, 3
    )
    return pl.pallas_call(
        finish_kernel,
        out_shape=[shape(volume.shape, f32), shape(measured.shape, f32)],
        in_specs=[VMEM] * 8,
        out_specs=[VMEM] * 2,
        scratch_shapes=[pltpu.VMEM((blocks, slices + 16, LANES), f32)],
        name="smooth",
    )(volume, first, turned, halo_in, sums, start, projected, later)


def solution(mesh):
    return jax.shard_map(
        functools.partial(shards, mesh.shape["tile"], mesh.shape["slab"]),
        mesh=mesh,
        in_specs=(
            P("slab", "tile"),
            P("slab", "tile"),
            P("slab", "tile"),
            P("tile", None, None),
            P("tile"),
            P("tile"),
        ),
        out_specs=(P("slab", "tile"), P("slab", "tile")),
        check_vma=False,
    )
```
